32 devices in a mesh: grp: 2 (over y), gene: 4 (over z), row: 4 (over x, core).
Axes of the slice: x: 2, y: 2, z: 4, core: 2. Of those that a mesh axis runs over, the one named last changes fastest.
Arguments:
- x_slab: bfloat16 [24576, 2560], P(('grp', 'row'), 'gene'), parts along dimension 0, may hold values from -6 to 6
- cell_factor: bfloat16 [4096, 128], P(('grp', 'row')), parts along dimension 0, may hold values from -1.5 to 1.5
- row_index: int32 [24576], P(('grp', 'row')), parts along dimension 0, may hold values from 0 to 2047, as said below
- gene_scale: float32 [5120], P(('grp', 'gene')), parts along dimension 0, may hold values from 0.3 to 3
- gene_factor: float32 [5120, 128], P(('grp', 'gene', 'row')), parts along dimension 0, may hold values from -1.5 to 1.5
- first_moment: float32 [5120, 128], P(('grp', 'gene', 'row')), parts along dimension 0, may hold values from -1.2 to 1.2
- second_moment: float32 [5120, 128], P(('grp', 'gene', 'row')), parts along dimension 0, may hold values from 0.05 to 1
Outputs:
- grad_cells: float32 [24576, 128], P(('grp', 'row', 'gene')), parts along dimension 0
- new_factor: float32 [5120, 128], P(('grp', 'gene', 'row')), parts along dimension 0
- new_first: float32 [5120, 128], P(('grp', 'gene', 'row')), parts along dimension 0
- new_second: float32 [5120, 128], P(('grp', 'gene', 'row')), parts along dimension 0
The draws below stay inside these ranges and needn't reach their ends.
There are 2 independent parts, one for each index of `grp`. The reference program is written for one: setup_inputs(seed, part) draws one part's arguments, and reference() takes and returns one part's arrays. A program takes and returns all parts, laid end to end along the dimension named above; each array names one. Nothing has to cross between parts.
Inputs may be any that keep to these rules, and one draw needn't show every extreme that they name: `row_index`: rows r * 3072 to (r + 1) * 3072 - 1 name cells r * 512 to (r + 1) * 512 - 1; cells may repeat.
All inputs are finite; a program needn't handle non-finite values.
Results may differ from the reference program's by a relative error of at most 0.008.
Values may be sent and summed in bfloat16 or wider, within the bound.
A program may use at most 64 MiB of HBM per device.

```python
import math
import jax
import jax.numpy as jnp
from jax import lax

R = 128
B_DEV = 3072
G_DEV = 640
CELLS_DEV = 512
B = 12288
G = 2560
CELLS = 2048


def draw_row_index(key, part):
    blocks = B // B_DEV
    key_a, key_b, key_c = jax.random.split(key, 3)
    local = jax.random.randint(key_a, (blocks, B_DEV), 0, CELLS_DEV)
    half = B_DEV // 2
    first_pos = jax.random.randint(key_b, (blocks,), 0, half)
    second_pos = half + jax.random.randint(key_c, (blocks,), 0, B_DEV - half)
    column = jnp.arange(B_DEV)[None, :]
    local = jnp.where(column == first_pos[:, None], 0, local)
    local = jnp.where(column == second_pos[:, None], CELLS_DEV - 1, local)
    offsets = jnp.arange(blocks) * CELLS_DEV
    return (local + offsets[:, None]).reshape(B).astype(jnp.int32)


def levels(own_key, shape, cuts, smallest, high):
    def one(axis_at, parts):
        heights = jax.random.uniform(jax.random.fold_in(jax.random.fold_in(own_key, 6), axis_at), (parts,), jnp.float32, smallest / len(cuts), high / len(cuts))
        return jnp.repeat(jnp.exp(heights), shape[axis_at] // parts).reshape((-1,) + (1,) * (len(shape) - axis_at - 1))

    level = one(*cuts[0])
    for cut in cuts[1:]:
        level = level * one(*cut)
    return level


def scatter_about(rng, extent, width, bound, cuts=(), kind=jnp.bfloat16):
    values = jax.random.normal(rng, extent, jnp.float32) * width
    if len(cuts) > 0:
        values = levels(rng, extent, cuts, -0.22, 0.18) * values
    return jnp.clip(values, min=-bound, max=bound).astype(kind)


def setup_inputs(seed: int = 0, part: int = 0) -> dict:
    streams_of = jax.random.split(jax.random.key(seed), 8)
    part_splits = jax.random.split(jax.random.fold_in(streams_of[7], part), 8)
    x_slab = scatter_about(part_splits[0], (B, G), 1.0, 6.0, ((0, 4), (1, 4)))
    cell_factor = scatter_about(part_splits[1], (CELLS, R), 0.25, 1.5, ((0, 4),))
    row_index = draw_row_index(jax.random.fold_in(jax.random.fold_in(streams_of[7], part), 71), part)
    gene_scale = jnp.clip(jnp.exp(math.log(3.0) - 2.3025851 * jax.random.uniform(part_splits[3], (G,), jnp.float32) ** levels(part_splits[3], (G,), ((0, 4),), -0.2, 0.2)), 0.3, 3.0)
    gene_factor = scatter_about(part_splits[4], (G, R), 0.25, 1.5, ((0, 16),), jnp.float32)
    first_moment = scatter_about(part_splits[5], (G, R), 0.2, 1.2, ((0, 16),), jnp.float32)
    second_moment = jnp.clip(jnp.exp(math.log(1.0) - 2.9957323 * jax.random.uniform(part_splits[6], (G, R), jnp.float32) ** levels(part_splits[6], (G, R), ((0, 16),), -0.2, 0.2)), 0.05, 1.0)
    return dict(x_slab=x_slab, cell_factor=cell_factor, row_index=row_index, gene_scale=gene_scale, gene_factor=gene_factor, first_moment=first_moment, second_moment=second_moment)


tukey_c = 4.685
beta_one = 0.9
beta_two = 0.999
learn_rate = 0.02
adam_eps = 1e-08

def influence(factors, x_part, factor_part, scale_part):
    pred = lax.dot_general(factors, factor_part, (((1,), (1,)), ((), ())), preferred_element_type=jnp.float32)
    resid = x_part.astype(jnp.float32) - pred
    scaled = resid / scale_part[None, :]
    ratio = scaled / tukey_c
    inside = 1.0 - ratio * ratio
    weight = jnp.where(jnp.abs(ratio) < 1.0, inside * inside, 0.0)
    return (scaled * weight / scale_part[None, :]).astype(jnp.bfloat16)

def reference(x_slab, cell_factor, row_index, gene_scale, gene_factor, first_moment, second_moment):
    factors = jnp.take(cell_factor, row_index.astype(jnp.int32), axis=0)
    factor_bf = gene_factor.astype(jnp.bfloat16)
    blocks = G // G_DEV
    x_blocks = x_slab.reshape(B, blocks, G_DEV).transpose(1, 0, 2)
    f_blocks = factor_bf.reshape(blocks, G_DEV, R)
    s_blocks = gene_scale.reshape(blocks, G_DEV)

    def one_block(total, items):
        x_part, f_part, s_part = items
        infl = influence(factors, x_part, f_part, s_part)
        total = total + jnp.dot(infl, f_part, preferred_element_type=jnp.float32)
        cols = lax.dot_general(infl, factors, (((0,), (0,)), ((), ())), preferred_element_type=jnp.float32)
        return (total, cols)
    grad_rows, cols = lax.scan(one_block, jnp.zeros((B, R), jnp.float32), (x_blocks, f_blocks, s_blocks))
    scale_k = 4.0 / math.sqrt(G)
    grad_cells = -scale_k * grad_rows
    grad_genes = -scale_k * cols.reshape(G, R)
    new_first = beta_one * first_moment + (1.0 - beta_one) * grad_genes
    new_second = beta_two * second_moment + (1.0 - beta_two) * grad_genes * grad_genes
    first_hat = new_first / (1.0 - beta_one ** 10)
    second_hat = new_second / (1.0 - beta_two ** 10)
    new_factor = gene_factor - learn_rate * first_hat / (jnp.sqrt(second_hat) + adam_eps)
    return (grad_cells, new_factor, new_first, new_second)
```

```python
import functools
import math

import jax
import jax.numpy as jnp
from jax import lax
from jax.experimental import pallas as pl
from jax.experimental.pallas import tpu as pltpu
from jax.sharding import PartitionSpec as P

tukey_c = 4.685
beta_one = 0.9
beta_two = 0.999
learn_rate = 0.02
adam_eps = 1e-08
MESH = pl.DeviceIdType.MESH
LANES = 128


def plan(rows, n_gene):
    per = rows // n_gene
    if per >= 256:
        chunk = 256 if per % 256 == 0 else per
        return per, chunk, per // chunk, 1
    group = max(g for g in range(1, n_gene + 1) if n_gene % g == 0 and g * per <= 384 and (g * per) % LANES == 0)
    return per, per * group, 1, group


def kernel(
    n_gene,
    n_row,
    x_hbm,
    cell_ref,
    index_ref,
    scale_ref,
    gene_ref,
    rows_out,
    genes_out,
    x_buf,
    fac,
    fac_t,
    gath,
    gath_t,
    cols,
    send_buf,
    recv_buf,
    own,
    col_send,
    col_recv,
    x_sem,
    ag_send_sem,
    ag_recv_sem,
    send_sem,
    recv_sem,
    col_send_sem,
    col_recv_sem,
):
    rows, genes = x_buf.shape
    cells, rank = cell_ref.shape
    genes_own = gene_ref.shape[0]
    per, chunk, pieces, group = plan(rows, n_gene)
    n_chunk = rows // chunk
    own_chunks = pieces
    me_gene = lax.axis_index("gene")
    me_row = lax.axis_index("row")

    barrier = pltpu.get_barrier_semaphore()
    for step in range(1, n_row):
        pl.semaphore_signal(barrier, inc=1, device_id={"row": lax.rem(me_row + step, n_row)}, device_id_type=MESH)
    for step in range(1, n_gene):
        pl.semaphore_signal(barrier, inc=1, device_id={"gene": lax.rem(me_gene + step, n_gene)}, device_id_type=MESH)

    if group == 1:
        first = me_gene * pieces + pieces
    else:
        first = me_gene // group + 1

    def chunk_at(i):
        return lax.rem(first + i, n_chunk)

    def x_copy(i):
        window = pl.ds(pl.multiple_of(chunk_at(i) * chunk, chunk), chunk)
        return pltpu.make_async_copy(x_hbm.at[window], x_buf.at[pl.ds(i * chunk, chunk)], x_sem.at[i])

    for i in range(n_chunk):
        x_copy(i).start()

    own_genes = pl.ds(pl.multiple_of(me_row * genes_own, genes_own), genes_own)
    gath[own_genes] = gene_ref[...].astype(jnp.bfloat16)

    cell_t = cell_ref[...].astype(jnp.float32).T.astype(jnp.bfloat16)
    cell_id = lax.broadcasted_iota(jnp.int32, (cells, LANES), 0) + me_row * cells

    def gather_factors(c):
        parts = []
        for k in range(chunk // LANES):
            at = c * (chunk // LANES) + k
            hit = (cell_id == index_ref[pl.ds(at, 1), :]).astype(jnp.float32).astype(jnp.bfloat16)
            parts.append(jnp.dot(cell_t, hit, preferred_element_type=jnp.float32))
        both = jnp.concatenate(parts, axis=1)
        fac_t[c] = both.astype(jnp.bfloat16)
        fac[c] = both.T.astype(jnp.bfloat16)

    half = n_chunk // 2
    for c in range(half):
        gather_factors(c)

    pl.semaphore_wait(barrier, n_row + n_gene - 2)

    def ag_copy(step):
        peer = lax.rem(me_row + step, n_row)
        return pltpu.make_async_remote_copy(
            src_ref=gath.at[own_genes],
            dst_ref=gath.at[own_genes],
            send_sem=ag_send_sem.at[step - 1],
            recv_sem=ag_recv_sem.at[step - 1],
            device_id={"row": peer},
            device_id_type=MESH,
        )

    for step in range(1, n_row):
        ag_copy(step).start()
    for c in range(half, n_chunk):
        gather_factors(c)
    inv = 1.0 / scale_ref[...]
    inv_tc = inv * (1.0 / tukey_c)
    inv_sq = inv * inv
    for step in range(1, n_row):
        ag_copy(step).wait()
    factor = gath[...]
    gath_t[...] = factor.astype(jnp.float32).T.astype(jnp.bfloat16)

    def block_copy(i, j):
        c = chunk_at(i)
        owner = c // pieces if group == 1 else c * group + j
        piece = lax.rem(c, pieces) if group == 1 else 0
        size = chunk if group == 1 else per
        return pltpu.make_async_remote_copy(
            src_ref=send_buf.at[i, pl.ds(j * size, size)],
            dst_ref=recv_buf.at[me_gene, piece],
            send_sem=send_sem.at[i, j],
            recv_sem=recv_sem.at[me_gene, piece],
            device_id={"gene": owner},
            device_id_type=MESH,
        )

    for i in range(n_chunk):
        c = chunk_at(i)
        x_copy(i).wait()
        f = fac[c]
        pred = jnp.dot(f, gath_t[...], preferred_element_type=jnp.float32)
        resid = x_buf[i * chunk : (i + 1) * chunk].astype(jnp.float32) - pred
        ratio = resid * inv_tc
        inside = jnp.maximum(1.0 - ratio * ratio, 0.0)
        infl = (resid * inv_sq * (inside * inside)).astype(jnp.bfloat16)
        part = jnp.dot(infl, gath[...], preferred_element_type=jnp.float32)
        if group == 1 and i >= n_chunk - own_chunks:
            own[i - (n_chunk - own_chunks)] = part
        else:
            send_buf[i] = part.astype(jnp.bfloat16)
            if group > 1:
                for j in range(group):

                    @pl.when(c * group + j == me_gene)
                    def _():
                        own[0] = part[j * per : (j + 1) * per]

        add = jnp.dot(fac_t[c], infl, preferred_element_type=jnp.float32)
        cols[...] = add if i == 0 else cols[...] + add
        if group == 1:
            if i < n_chunk - own_chunks:
                block_copy(i, 0).start()
        else:
            for j in range(group):

                @pl.when(c * group + j != me_gene)
                def _():
                    block_copy(i, j).start()

    total = cols[...].T
    col_send[...] = total.astype(jnp.bfloat16)
    cols_own = jnp.zeros((genes_own, rank), jnp.float32)

    def col_copy(step):
        peer = lax.rem(me_row + step, n_row)
        return pltpu.make_async_remote_copy(
            src_ref=col_send.at[pl.ds(pl.multiple_of(peer * genes_own, genes_own), genes_own)],
            dst_ref=col_recv.at[step - 1],
            send_sem=col_send_sem.at[step - 1],
            recv_sem=col_recv_sem.at[step - 1],
            device_id={"row": peer},
            device_id_type=MESH,
        )

    for step in range(1, n_row):
        col_copy(step).start()
    cols_own = col_send[own_genes].astype(jnp.float32)
    for step in range(1, n_row):
        col_copy(step).wait()
        cols_own = cols_own + col_recv[step - 1].astype(jnp.float32)
    genes_out[...] = cols_own

    size = chunk if group == 1 else per

    def arrived(step, piece):
        sender = lax.rem(me_gene + n_gene - step, n_gene)
        copy = pltpu.make_async_remote_copy(
            src_ref=recv_buf.at[sender, piece],
            dst_ref=recv_buf.at[sender, piece],
            send_sem=send_sem.at[0, 0],
            recv_sem=recv_sem.at[sender, piece],
            device_id={"gene": sender},
            device_id_type=MESH,
        )
        copy.wait_recv()
        return recv_buf[sender, piece].astype(jnp.float32)

    for piece in range(pieces):
        acc = own[piece]
        for step in range(1, n_gene):
            acc = acc + arrived(step, piece)
        rows_out[piece * size : (piece + 1) * size] = acc

    for i in range(n_chunk):
        if group == 1:
            if i < n_chunk - own_chunks:
                block_copy(i, 0).wait_send()
        else:
            for j in range(group):

                @pl.when(chunk_at(i) * group + j != me_gene)
                def _():
                    block_copy(i, j).wait_send()


def fused(n_gene, n_row, x_slab, cell_factor, index, scale, gene_factor):
    rows, genes = x_slab.shape
    cells, rank = cell_factor.shape
    genes_own = gene_factor.shape[0]
    per, chunk, pieces, group = plan(rows, n_gene)
    n_chunk = rows // chunk
    size = chunk if group == 1 else per
    vmem = pl.BlockSpec(memory_space=pltpu.VMEM)
    bf = jnp.bfloat16
    dma = pltpu.SemaphoreType.DMA
    return pl.pallas_call(
        functools.partial(kernel, n_gene, n_row),
        out_shape=(
            jax.ShapeDtypeStruct((per, rank), jnp.float32),
            jax.ShapeDtypeStruct((genes_own, rank), jnp.float32),
        ),
        in_specs=[pl.BlockSpec(memory_space=pl.ANY), vmem, vmem, vmem, vmem],
        out_specs=(vmem, vmem),
        scratch_shapes=[
            pltpu.VMEM((rows, genes), bf),
            pltpu.VMEM((n_chunk, chunk, rank), bf),
            pltpu.VMEM((n_chunk, rank, chunk), bf),
            pltpu.VMEM((genes, rank), bf),
            pltpu.VMEM((rank, genes), bf),
            pltpu.VMEM((rank, genes), jnp.float32),
            pltpu.VMEM((n_chunk, chunk, rank), bf),
            pltpu.VMEM((n_gene, pieces, size, rank), bf),
            pltpu.VMEM((pieces, size, rank), jnp.float32),
            pltpu.VMEM((genes, rank), bf),
            pltpu.VMEM((n_row - 1, genes_own, rank), bf),
            dma((n_chunk,)),
            dma((n_row - 1,)),
            dma((n_row - 1,)),
            dma((n_chunk, group)),
            dma((n_gene, pieces)),
            dma((n_row - 1,)),
            dma((n_row - 1,)),
        ],
        compiler_params=pltpu.CompilerParams(collective_id=0, has_side_effects=True),
    )(x_slab, cell_factor, index, scale, gene_factor)


def local(x_slab, cell_factor, row_index, gene_scale, gene_factor, first_moment, second_moment):
    rows_dev, genes_dev = x_slab.shape
    n_gene = lax.axis_size("gene")
    n_row = lax.axis_size("row")
    scale_k = 4.0 / math.sqrt(genes_dev * n_gene)
    grad_rows, grad_cols = fused(
        n_gene,
        n_row,
        x_slab,
        cell_factor,
        row_index.reshape(rows_dev // LANES, LANES),
        gene_scale.reshape(1, genes_dev),
        gene_factor,
    )
    grad_cells = -scale_k * grad_rows
    grad_genes = -scale_k * grad_cols
    new_first = beta_one * first_moment + (1.0 - beta_one) * grad_genes
    new_second = beta_two * second_moment + (1.0 - beta_two) * grad_genes * grad_genes
    first_hat = new_first / (1.0 - beta_one**10)
    second_hat = new_second / (1.0 - beta_two**10)
    new_factor = gene_factor - learn_rate * first_hat / (jnp.sqrt(second_hat) + adam_eps)
    return (grad_cells, new_factor, new_first, new_second)


def solution(mesh):
    in_specs = (
        P(("grp", "row"), "gene"),
        P(("grp", "row"), None),
        P(("grp", "row")),
        P(("grp", "gene")),
        P(("grp", "gene", "row"), None),
        P(("grp", "gene", "row"), None),
        P(("grp", "gene", "row"), None),
    )
    out_specs = (
        P(("grp", "row", "gene"), None),
        P(("grp", "gene", "row"), None),
        P(("grp", "gene", "row"), None),
        P(("grp", "gene", "row"), None),
    )
    return jax.shard_map(local, mesh=mesh, in_specs=in_specs, out_specs=out_specs, check_vma=False)
```

```python
import functools
import math

import jax
import jax.numpy as jnp
from jax import lax
from jax.experimental import pallas as pl
from jax.experimental.pallas import tpu as pltpu
from jax.sharding import PartitionSpec as P

tukey_c = 4.685
beta_one = 0.9
beta_two = 0.999
learn_rate = 0.02
adam_eps = 1e-08
MESH = pl.DeviceIdType.MESH
LANES = 128


def plan(rows, n_gene):
    per = rows // n_gene
    if per >= 256:
        chunk = 256 if per % 256 == 0 else per
        return per, chunk, per // chunk, 1
    group = max(g for g in range(1, n_gene + 1) if n_gene % g == 0 and g * per <= 384 and (g * per) % LANES == 0)
    return per, per * group, 1, group


def kernel(
    n_gene,
    n_row,
    x_hbm,
    cell_hbm,
    index_hbm,
    scale_hbm,
    gene_hbm,
    first_hbm,
    second_hbm,
    rows_out,
    factor_out,
    first_out,
    second_out,
    cell_ref,
    index_ref,
    scale_ref,
    gene_ref,
    first_ref,
    second_ref,
    x_buf,
    fac,
    fac_t,
    gath,
    gath_t,
    cols,
    send_buf,
    recv_buf,
    own,
    col_send,
    col_recv,
    load_sem,
    x_sem,
    ag_send_sem,
    ag_recv_sem,
    send_sem,
    recv_sem,
    col_send_sem,
    col_recv_sem,
):
    rows, genes = x_buf.shape
    cells, rank = cell_ref.shape
    genes_own = gene_ref.shape[0]
    scale_k = 4.0 / math.sqrt(genes * n_gene)
    per, chunk, pieces, group = plan(rows, n_gene)
    n_chunk = rows // chunk
    own_chunks = pieces
    me_gene = lax.axis_index("gene")
    me_row = lax.axis_index("row")

    barrier = pltpu.get_barrier_semaphore()
    for step in range(1, n_row):
        pl.semaphore_signal(barrier, inc=1, device_id={"row": lax.rem(me_row + step, n_row)}, device_id_type=MESH)
    for step in range(1, n_gene):
        pl.semaphore_signal(barrier, inc=1, device_id={"gene": lax.rem(me_gene + step, n_gene)}, device_id_type=MESH)

    if group == 1:
        first = me_gene * pieces + pieces
    else:
        first = me_gene // group + 1

    def chunk_at(i):
        return lax.rem(first + i, n_chunk)

    def x_copy(i):
        window = pl.ds(pl.multiple_of(chunk_at(i) * chunk, chunk), chunk)
        return pltpu.make_async_copy(x_hbm.at[window], x_buf.at[pl.ds(i * chunk, chunk)], x_sem.at[i])

    loads = [
        pltpu.make_async_copy(src, dst, load_sem.at[k])
        for k, (src, dst) in enumerate(
            (
                (gene_hbm, gene_ref),
                (cell_hbm, cell_ref),
                (index_hbm, index_ref),
                (scale_hbm, scale_ref),
                (first_hbm, first_ref),
                (second_hbm, second_ref),
            )
        )
    ]
    for load in loads[:4]:
        load.start()
    for i in range(n_chunk):
        x_copy(i).start()
    for load in loads[4:]:
        load.start()

    loads[0].wait()
    own_genes = pl.ds(pl.multiple_of(me_row * genes_own, genes_own), genes_own)
    gath[own_genes] = gene_ref[...].astype(jnp.bfloat16)

    loads[1].wait()
    loads[2].wait()
    cell_t = cell_ref[...].astype(jnp.float32).T.astype(jnp.bfloat16)
    cell_id = lax.broadcasted_iota(jnp.int32, (cells, LANES), 0) + me_row * cells

    def gather_factors(c):
        parts = []
        for k in range(chunk // LANES):
            at = c * (chunk // LANES) + k
            hit = (cell_id == index_ref[pl.ds(at, 1), :]).astype(jnp.float32).astype(jnp.bfloat16)
            parts.append(jnp.dot(cell_t, hit, preferred_element_type=jnp.float32))
        both = jnp.concatenate(parts, axis=1)
        fac_t[c] = both.astype(jnp.bfloat16)
        fac[c] = both.T.astype(jnp.bfloat16)

    half = n_chunk // 2
    for c in range(half):
        gather_factors(c)

    pl.semaphore_wait(barrier, n_row + n_gene - 2)

    def ag_copy(step):
        peer = lax.rem(me_row + step, n_row)
        return pltpu.make_async_remote_copy(
            src_ref=gath.at[own_genes],
            dst_ref=gath.at[own_genes],
            send_sem=ag_send_sem.at[step - 1],
            recv_sem=ag_recv_sem.at[step - 1],
            device_id={"row": peer},
            device_id_type=MESH,
        )

    for step in range(1, n_row):
        ag_copy(step).start()
    for c in range(half, n_chunk):
        gather_factors(c)
    loads[3].wait()
    scale = jnp.concatenate([scale_ref[k : k + 1, :] for k in range(genes // LANES)], axis=1)
    inv = 1.0 / scale
    inv_tc = inv * (1.0 / tukey_c)
    inv_sq = inv * inv
    for step in range(1, n_row):
        ag_copy(step).wait()
    factor = gath[...]
    gath_t[...] = factor.astype(jnp.float32).T.astype(jnp.bfloat16)

    def block_copy(i, j):
        c = chunk_at(i)
        owner = c // pieces if group == 1 else c * group + j
        piece = lax.rem(c, pieces) if group == 1 else 0
        size = chunk if group == 1 else per
        return pltpu.make_async_remote_copy(
            src_ref=send_buf.at[i, pl.ds(j * size, size)],
            dst_ref=recv_buf.at[me_gene, piece],
            send_sem=send_sem.at[i, j],
            recv_sem=recv_sem.at[me_gene, piece],
            device_id={"gene": owner},
            device_id_type=MESH,
        )

    for i in range(n_chunk):
        c = chunk_at(i)
        x_copy(i).wait()
        f = fac[c]
        pred = jnp.dot(f, gath_t[...], preferred_element_type=jnp.float32)
        resid = x_buf[i * chunk : (i + 1) * chunk].astype(jnp.float32) - pred
        ratio = resid * inv_tc
        inside = jnp.maximum(1.0 - ratio * ratio, 0.0)
        infl = (resid * inv_sq * (inside * inside)).astype(jnp.bfloat16)
        part = jnp.dot(infl, gath[...], preferred_element_type=jnp.float32)
        if group == 1 and i >= n_chunk - own_chunks:
            own[i - (n_chunk - own_chunks)] = part
        else:
            send_buf[i] = part.astype(jnp.bfloat16)
            if group > 1:
                for j in range(group):

                    @pl.when(c * group + j == me_gene)
                    def _():
                        own[0] = part[j * per : (j + 1) * per]

        add = jnp.dot(fac_t[c], infl, preferred_element_type=jnp.float32)
        cols[...] = add if i == 0 else cols[...] + add
        if group == 1:
            if i < n_chunk - own_chunks:
                block_copy(i, 0).start()
        else:
            for j in range(group):

                @pl.when(c * group + j != me_gene)
                def _():
                    block_copy(i, j).start()

    total = cols[...].T
    col_send[...] = total.astype(jnp.bfloat16)
    cols_own = jnp.zeros((genes_own, rank), jnp.float32)

    def col_copy(step):
        peer = lax.rem(me_row + step, n_row)
        return pltpu.make_async_remote_copy(
            src_ref=col_send.at[pl.ds(pl.multiple_of(peer * genes_own, genes_own), genes_own)],
            dst_ref=col_recv.at[step - 1],
            send_sem=col_send_sem.at[step - 1],
            recv_sem=col_recv_sem.at[step - 1],
            device_id={"row": peer},
            device_id_type=MESH,
        )

    for step in range(1, n_row):
        col_copy(step).start()
    cols_own = col_send[own_genes].astype(jnp.float32)
    for step in range(1, n_row):
        col_copy(step).wait()
        cols_own = cols_own + col_recv[step - 1].astype(jnp.float32)
    loads[4].wait()
    loads[5].wait()
    grad_genes = -scale_k * cols_own
    new_first = beta_one * first_ref[...] + (1.0 - beta_one) * grad_genes
    new_second = beta_two * second_ref[...] + (1.0 - beta_two) * grad_genes * grad_genes
    first_hat = new_first / (1.0 - beta_one**10)
    second_hat = new_second / (1.0 - beta_two**10)
    first_out[...] = new_first
    second_out[...] = new_second
    factor_out[...] = gene_ref[...] - learn_rate * first_hat / (jnp.sqrt(second_hat) + adam_eps)

    size = chunk if group == 1 else per

    def arrived(step, piece):
        sender = lax.rem(me_gene + n_gene - step, n_gene)
        copy = pltpu.make_async_remote_copy(
            src_ref=recv_buf.at[sender, piece],
            dst_ref=recv_buf.at[sender, piece],
            send_sem=send_sem.at[0, 0],
            recv_sem=recv_sem.at[sender, piece],
            device_id={"gene": sender},
            device_id_type=MESH,
        )
        copy.wait_recv()
        return recv_buf[sender, piece].astype(jnp.float32)

    for piece in range(pieces):
        acc = own[piece]
        for step in range(1, n_gene):
            acc = acc + arrived(step, piece)
        rows_out[piece * size : (piece + 1) * size] = -scale_k * acc

    for i in range(n_chunk):
        if group == 1:
            if i < n_chunk - own_chunks:
                block_copy(i, 0).wait_send()
        else:
            for j in range(group):

                @pl.when(chunk_at(i) * group + j != me_gene)
                def _():
                    block_copy(i, j).wait_send()


def fused(n_gene, n_row, x_slab, cell_factor, index, scale, gene_factor, first, second):
    rows, genes = x_slab.shape
    cells, rank = cell_factor.shape
    genes_own = gene_factor.shape[0]
    per, chunk, pieces, group = plan(rows, n_gene)
    n_chunk = rows // chunk
    size = chunk if group == 1 else per
    vmem = pl.BlockSpec(memory_space=pltpu.VMEM)
    bf = jnp.bfloat16
    dma = pltpu.SemaphoreType.DMA
    return pl.pallas_call(
        functools.partial(kernel, n_gene, n_row),
        out_shape=(pltpu.VMEM((per, rank), jnp.float32),) + (pltpu.VMEM((genes_own, rank), jnp.float32),) * 3,
        in_specs=[pl.BlockSpec(memory_space=pl.ANY)] * 7,
        out_specs=(vmem,) * 4,
        scratch_shapes=[
            pltpu.VMEM(cell_factor.shape, bf),
            pltpu.VMEM(index.shape, jnp.int32),
            pltpu.VMEM(scale.shape, jnp.float32),
            pltpu.VMEM(gene_factor.shape, jnp.float32),
            pltpu.VMEM(gene_factor.shape, jnp.float32),
            pltpu.VMEM(gene_factor.shape, jnp.float32),
            pltpu.VMEM((rows, genes), bf),
            pltpu.VMEM((n_chunk, chunk, rank), bf),
            pltpu.VMEM((n_chunk, rank, chunk), bf),
            pltpu.VMEM((genes, rank), bf),
            pltpu.VMEM((rank, genes), bf),
            pltpu.VMEM((rank, genes), jnp.float32),
            pltpu.VMEM((n_chunk, chunk, rank), bf),
            pltpu.VMEM((n_gene, pieces, size, rank), bf),
            pltpu.VMEM((pieces, size, rank), jnp.float32),
            pltpu.VMEM((genes, rank), bf),
            pltpu.VMEM((n_row - 1, genes_own, rank), bf),
            dma((6,)),
            dma((n_chunk,)),
            dma((n_row - 1,)),
            dma((n_row - 1,)),
            dma((n_chunk, group)),
            dma((n_gene, pieces)),
            dma((n_row - 1,)),
            dma((n_row - 1,)),
        ],
        compiler_params=pltpu.CompilerParams(collective_id=0, has_side_effects=True),
    )(x_slab, cell_factor, index, scale, gene_factor, first, second)


def write_kernel(*refs):
    count = (len(refs) - 1) // 2
    sem = refs[-1]
    copies = [pltpu.make_async_copy(refs[k], refs[count + k], sem.at[k]) for k in range(count)]
    for copy in copies:
        copy.start()
    for copy in copies:
        copy.wait()


def write_out(held):
    return pl.pallas_call(
        write_kernel,
        out_shape=tuple(jax.ShapeDtypeStruct(h.shape, h.dtype) for h in held),
        in_specs=[pl.BlockSpec(memory_space=pltpu.VMEM)] * len(held),
        out_specs=(pl.BlockSpec(memory_space=pl.ANY),) * len(held),
        scratch_shapes=[pltpu.SemaphoreType.DMA((len(held),))],
    )(*[pltpu.with_memory_space_constraint(h, pltpu.VMEM) for h in held])


def local(x_slab, cell_factor, row_index, gene_scale, gene_factor, first_moment, second_moment):
    rows_dev, genes_dev = x_slab.shape
    n_gene = lax.axis_size("gene")
    n_row = lax.axis_size("row")
    held = fused(
        n_gene,
        n_row,
        x_slab,
        cell_factor,
        row_index.reshape(rows_dev // LANES, LANES),
        gene_scale.reshape(genes_dev // LANES, LANES),
        gene_factor,
        first_moment,
        second_moment,
    )
    return write_out(held)


def solution(mesh):
    in_specs = (
        P(("grp", "row"), "gene"),
        P(("grp", "row"), None),
        P(("grp", "row")),
        P(("grp", "gene")),
        P(("grp", "gene", "row"), None),
        P(("grp", "gene", "row"), None),
        P(("grp", "gene", "row"), None),
    )
    out_specs = (
        P(("grp", "row", "gene"), None),
        P(("grp", "gene", "row"), None),
        P(("grp", "gene", "row"), None),
        P(("grp", "gene", "row"), None),
    )
    return jax.shard_map(local, mesh=mesh, in_specs=in_specs, out_specs=out_specs, check_vma=False)
```

```python
import functools
import math

import jax
import jax.numpy as jnp
from jax import lax
from jax.experimental import pallas as pl
from jax.experimental.pallas import tpu as pltpu
from jax.sharding import PartitionSpec as P

tukey_c = 4.685
beta_one = 0.9
beta_two = 0.999
learn_rate = 0.02
adam_eps = 1e-08
MESH = pl.DeviceIdType.MESH
LANES = 128


def plan(rows, n_gene):
    per = rows // n_gene
    if per >= 256:
        chunk = 256 if per % 256 == 0 else per
        return per, chunk, per // chunk, 1
    group = max(g for g in range(1, n_gene + 1) if n_gene % g == 0 and g * per <= 384 and (g * per) % LANES == 0)
    return per, per * group, 1, group


def kernel(
    n_gene,
    n_row,
    x_hbm,
    cell_hbm,
    index_hbm,
    scale_hbm,
    gene_hbm,
    first_hbm,
    second_hbm,
    rows_out,
    factor_out,
    first_out,
    second_out,
    cell_ref,
    index_ref,
    scale_ref,
    gene_ref,
    first_ref,
    second_ref,
    x_buf,
    fac,
    fac_t,
    gath,
    gath_t,
    cols,
    send_buf,
    recv_buf,
    own,
    col_send,
    col_recv,
    load_sem,
    x_sem,
    ag_send_sem,
    ag_recv_sem,
    send_sem,
    recv_sem,
    col_send_sem,
    col_recv_sem,
):
    rows, genes = x_buf.shape
    cells, rank = cell_ref.shape
    genes_own = gene_ref.shape[0]
    scale_k = 4.0 / math.sqrt(genes * n_gene)
    per, chunk, pieces, group = plan(rows, n_gene)
    n_chunk = rows // chunk
    own_chunks = pieces
    me_gene = lax.axis_index("gene")
    me_row = lax.axis_index("row")

    barrier = pltpu.get_barrier_semaphore()
    for step in range(1, n_row):
        pl.semaphore_signal(barrier, inc=1, device_id={"row": lax.rem(me_row + step, n_row)}, device_id_type=MESH)
    relay = n_gene == 4 and group == 1
    if relay:
        high, low = me_gene // 2, lax.rem(me_gene, 2)
        inner = high + low - 2 * high * low
        outer = 1 - inner

        def partner(mask):
            flipped_high = 1 - high if mask >= 2 else high
            flipped_low = 1 - low if mask % 2 == 1 else low
            return 2 * flipped_high + flipped_low

        for mask in (1, 2):
            pl.semaphore_signal(barrier, inc=1, device_id={"gene": partner(mask)}, device_id_type=MESH)

        @pl.when(inner == 1)
        def _():
            pl.semaphore_signal(barrier, inc=1, device_id={"gene": partner(3)}, device_id_type=MESH)

        arrivals = n_row - 1 + 2 + inner
    else:
        for step in range(1, n_gene):
            peer = lax.rem(me_gene + step, n_gene)
            pl.semaphore_signal(barrier, inc=1, device_id={"gene": peer}, device_id_type=MESH)
        arrivals = n_row - 1 + n_gene - 1

    if group == 1:
        first = me_gene * pieces + pieces
    else:
        first = me_gene // group + 1

    def chunk_at(i):
        if relay:
            return partner(3 - i // pieces) * pieces + i % pieces
        return lax.rem(first + i, n_chunk)

    def x_copy(i):
        window = pl.ds(pl.multiple_of(chunk_at(i) * chunk, chunk), chunk)
        return pltpu.make_async_copy(x_hbm.at[window], x_buf.at[pl.ds(i * chunk, chunk)], x_sem.at[i])

    loads = [
        pltpu.make_async_copy(src, dst, load_sem.at[k])
        for k, (src, dst) in enumerate(
            (
                (gene_hbm, gene_ref),
                (cell_hbm, cell_ref),
                (index_hbm, index_ref),
                (scale_hbm, scale_ref),
                (first_hbm, first_ref),
                (second_hbm, second_ref),
            )
        )
    ]
    for load in loads[:4]:
        load.start()
    for i in range(n_chunk):
        x_copy(i).start()
    for load in loads[4:]:
        load.start()

    loads[0].wait()
    own_genes = pl.ds(pl.multiple_of(me_row * genes_own, genes_own), genes_own)
    gath[own_genes] = gene_ref[...].astype(jnp.bfloat16)

    loads[1].wait()
    loads[2].wait()
    cell_t = cell_ref[...].astype(jnp.float32).T.astype(jnp.bfloat16)
    cell_id = lax.broadcasted_iota(jnp.int32, (cells, LANES), 0) + me_row * cells

    def gather_factors(c):
        parts = []
        for k in range(chunk // LANES):
            at = c * (chunk // LANES) + k
            hit = (cell_id == index_ref[pl.ds(at, 1), :]).astype(jnp.float32).astype(jnp.bfloat16)
            parts.append(jnp.dot(cell_t, hit, preferred_element_type=jnp.float32))
        both = jnp.concatenate(parts, axis=1)
        fac_t[c] = both.astype(jnp.bfloat16)
        fac[c] = both.T.astype(jnp.bfloat16)

    half = n_chunk // 2
    for c in range(half):
        gather_factors(c)

    pl.semaphore_wait(barrier, arrivals)

    def ag_copy(step):
        peer = lax.rem(me_row + step, n_row)
        return pltpu.make_async_remote_copy(
            src_ref=gath.at[own_genes],
            dst_ref=gath.at[own_genes],
            send_sem=ag_send_sem.at[step - 1],
            recv_sem=ag_recv_sem.at[step - 1],
            device_id={"row": peer},
            device_id_type=MESH,
        )

    for step in range(1, n_row):
        ag_copy(step).start()
    for c in range(half, n_chunk):
        gather_factors(c)
    loads[3].wait()
    scale = jnp.concatenate([scale_ref[k : k + 1, :] for k in range(genes // LANES)], axis=1)
    inv = 1.0 / scale
    inv_tc = inv * (1.0 / tukey_c)
    inv_sq = inv * inv
    for step in range(1, n_row):
        ag_copy(step).wait()
    factor = gath[...]
    gath_t[...] = factor.astype(jnp.float32).T.astype(jnp.bfloat16)

    def block_copy(i, j):
        if relay:
            turn, piece = i // pieces, i % pieces
            target, slot = partner(3 - turn), turn
            if turn == 0:
                target, slot = outer * partner(1) + inner * target, 3 * outer
            return pltpu.make_async_remote_copy(
                src_ref=send_buf.at[i],
                dst_ref=recv_buf.at[slot, piece],
                send_sem=send_sem.at[i, 0],
                recv_sem=recv_sem.at[slot, piece],
                device_id={"gene": target},
                device_id_type=MESH,
            )
        c = chunk_at(i)
        owner = c // pieces if group == 1 else c * group + j
        piece = lax.rem(c, pieces) if group == 1 else 0
        size = chunk if group == 1 else per
        return pltpu.make_async_remote_copy(
            src_ref=send_buf.at[i, pl.ds(j * size, size)],
            dst_ref=recv_buf.at[me_gene, piece],
            send_sem=send_sem.at[i, j],
            recv_sem=recv_sem.at[me_gene, piece],
            device_id={"gene": owner},
            device_id_type=MESH,
        )

    def landed(slot, piece):
        pltpu.make_async_remote_copy(
            src_ref=recv_buf.at[slot, piece],
            dst_ref=recv_buf.at[slot, piece],
            send_sem=send_sem.at[0, 0],
            recv_sem=recv_sem.at[slot, piece],
            device_id={"gene": lax.rem(me_gene + 1, n_gene)},
            device_id_type=MESH,
        ).wait_recv()
        return recv_buf[slot, piece].astype(jnp.float32)

    for i in range(n_chunk):
        c = chunk_at(i)
        x_copy(i).wait()
        f = fac[c]
        pred = jnp.dot(f, gath_t[...], preferred_element_type=jnp.float32)
        resid = x_buf[i * chunk : (i + 1) * chunk].astype(jnp.float32) - pred
        ratio = resid * inv_tc
        inside = jnp.maximum(1.0 - ratio * ratio, 0.0)
        infl = (resid * inv_sq * (inside * inside)).astype(jnp.bfloat16)
        part = jnp.dot(infl, gath[...], preferred_element_type=jnp.float32)
        if group == 1 and i >= n_chunk - own_chunks:
            own[i - (n_chunk - own_chunks)] = part
        elif relay and i // pieces == 1:

            @pl.when(inner == 1)
            def _():
                send_buf[i] = (part + landed(3, i % pieces)).astype(jnp.bfloat16)

            @pl.when(inner == 0)
            def _():
                send_buf[i] = part.astype(jnp.bfloat16)

        else:
            send_buf[i] = part.astype(jnp.bfloat16)
            if group > 1:
                for j in range(group):

                    @pl.when(c * group + j == me_gene)
                    def _():
                        own[0] = part[j * per : (j + 1) * per]

        add = jnp.dot(fac_t[c], infl, preferred_element_type=jnp.float32)
        cols[...] = add if i == 0 else cols[...] + add
        if group == 1:
            if i < n_chunk - own_chunks:
                block_copy(i, 0).start()
        else:
            for j in range(group):

                @pl.when(c * group + j != me_gene)
                def _():
                    block_copy(i, j).start()

    total = cols[...].T
    col_send[...] = total.astype(jnp.bfloat16)
    cols_own = jnp.zeros((genes_own, rank), jnp.float32)

    def col_copy(step):
        peer = lax.rem(me_row + step, n_row)
        return pltpu.make_async_remote_copy(
            src_ref=col_send.at[pl.ds(pl.multiple_of(peer * genes_own, genes_own), genes_own)],
            dst_ref=col_recv.at[step - 1],
            send_sem=col_send_sem.at[step - 1],
            recv_sem=col_recv_sem.at[step - 1],
            device_id={"row": peer},
            device_id_type=MESH,
        )

    for step in range(1, n_row):
        col_copy(step).start()
    cols_own = col_send[own_genes].astype(jnp.float32)
    for step in range(1, n_row):
        col_copy(step).wait()
        cols_own = cols_own + col_recv[step - 1].astype(jnp.float32)
    loads[4].wait()
    loads[5].wait()
    grad_genes = -scale_k * cols_own
    new_first = beta_one * first_ref[...] + (1.0 - beta_one) * grad_genes
    new_second = beta_two * second_ref[...] + (1.0 - beta_two) * grad_genes * grad_genes
    first_hat = new_first / (1.0 - beta_one**10)
    second_hat = new_second / (1.0 - beta_two**10)
    first_out[...] = new_first
    second_out[...] = new_second
    factor_out[...] = gene_ref[...] - learn_rate * first_hat / (jnp.sqrt(second_hat) + adam_eps)

    size = chunk if group == 1 else per

    for piece in range(pieces):
        window = pl.ds(piece * size, size)
        acc = own[piece]
        if relay:
            acc = acc + landed(1, piece) + landed(2, piece)
            rows_out[window] = -scale_k * acc

            @pl.when(inner == 1)
            def _():
                rows_out[window] = -scale_k * (acc + landed(0, piece))
        else:
            for step in range(1, n_gene):
                acc = acc + landed(lax.rem(me_gene + n_gene - step, n_gene), piece)
            rows_out[window] = -scale_k * acc

    for i in range(n_chunk):
        if group == 1:
            if i < n_chunk - own_chunks:
                block_copy(i, 0).wait_send()
        else:
            for j in range(group):

                @pl.when(chunk_at(i) * group + j != me_gene)
                def _():
                    block_copy(i, j).wait_send()


def fused(n_gene, n_row, x_slab, cell_factor, index, scale, gene_factor, first, second):
    rows, genes = x_slab.shape
    cells, rank = cell_factor.shape
    genes_own = gene_factor.shape[0]
    per, chunk, pieces, group = plan(rows, n_gene)
    n_chunk = rows // chunk
    size = chunk if group == 1 else per
    vmem = pl.BlockSpec(memory_space=pltpu.VMEM)
    bf = jnp.bfloat16
    dma = pltpu.SemaphoreType.DMA
    return pl.pallas_call(
        functools.partial(kernel, n_gene, n_row),
        out_shape=(pltpu.VMEM((per, rank), jnp.float32),) + (pltpu.VMEM((genes_own, rank), jnp.float32),) * 3,
        in_specs=[pl.BlockSpec(memory_space=pl.ANY)] * 7,
        out_specs=(vmem,) * 4,
        scratch_shapes=[
            pltpu.VMEM(cell_factor.shape, bf),
            pltpu.VMEM(index.shape, jnp.int32),
            pltpu.VMEM(scale.shape, jnp.float32),
            pltpu.VMEM(gene_factor.shape, jnp.float32),
            pltpu.VMEM(gene_factor.shape, jnp.float32),
            pltpu.VMEM(gene_factor.shape, jnp.float32),
            pltpu.VMEM((rows, genes), bf),
            pltpu.VMEM((n_chunk, chunk, rank), bf),
            pltpu.VMEM((n_chunk, rank, chunk), bf),
            pltpu.VMEM((genes, rank), bf),
            pltpu.VMEM((rank, genes), bf),
            pltpu.VMEM((rank, genes), jnp.float32),
            pltpu.VMEM((n_chunk, chunk, rank), bf),
            pltpu.VMEM((n_gene, pieces, size, rank), bf),
            pltpu.VMEM((pieces, size, rank), jnp.float32),
            pltpu.VMEM((genes, rank), bf),
            pltpu.VMEM((n_row - 1, genes_own, rank), bf),
            dma((6,)),
            dma((n_chunk,)),
            dma((n_row - 1,)),
            dma((n_row - 1,)),
            dma((n_chunk, group)),
            dma((n_gene, pieces)),
            dma((n_row - 1,)),
            dma((n_row - 1,)),
        ],
        compiler_params=pltpu.CompilerParams(collective_id=0, has_side_effects=True),
    )(x_slab, cell_factor, index, scale, gene_factor, first, second)


def write_kernel(*refs):
    count = (len(refs) - 1) // 2
    sem = refs[-1]
    copies = [pltpu.make_async_copy(refs[k], refs[count + k], sem.at[k]) for k in range(count)]
    for copy in copies:
        copy.start()
    for copy in copies:
        copy.wait()


def write_out(held):
    return pl.pallas_call(
        write_kernel,
        out_shape=tuple(jax.ShapeDtypeStruct(h.shape, h.dtype) for h in held),
        in_specs=[pl.BlockSpec(memory_space=pltpu.VMEM)] * len(held),
        out_specs=(pl.BlockSpec(memory_space=pl.ANY),) * len(held),
        scratch_shapes=[pltpu.SemaphoreType.DMA((len(held),))],
    )(*[pltpu.with_memory_space_constraint(h, pltpu.VMEM) for h in held])


def local(x_slab, cell_factor, row_index, gene_scale, gene_factor, first_moment, second_moment):
    rows_dev, genes_dev = x_slab.shape
    n_gene = lax.axis_size("gene")
    n_row = lax.axis_size("row")
    held = fused(
        n_gene,
        n_row,
        x_slab,
        cell_factor,
        row_index.reshape(rows_dev // LANES, LANES),
        gene_scale.reshape(genes_dev // LANES, LANES),
        gene_factor,
        first_moment,
        second_moment,
    )
    return write_out(held)


def solution(mesh):
    in_specs = (
        P(("grp", "row"), "gene"),
        P(("grp", "row"), None),
        P(("grp", "row")),
        P(("grp", "gene")),
        P(("grp", "gene", "row"), None),
        P(("grp", "gene", "row"), None),
        P(("grp", "gene", "row"), None),
    )
    out_specs = (
        P(("grp", "row", "gene"), None),
        P(("grp", "gene", "row"), None),
        P(("grp", "gene", "row"), None),
        P(("grp", "gene", "row"), None),
    )
    return jax.shard_map(local, mesh=mesh, in_specs=in_specs, out_specs=out_specs, check_vma=False)
```

```python
import functools
import math

import jax
import jax.numpy as jnp
from jax import lax
from jax.experimental import pallas as pl
from jax.experimental.pallas import tpu as pltpu
from jax.sharding import PartitionSpec as P

tukey_c = 4.685
beta_one = 0.9
beta_two = 0.999
learn_rate = 0.02
adam_eps = 1e-08
MESH = pl.DeviceIdType.MESH
LANES = 128


def plan(rows, n_gene):
    per = rows // n_gene
    if per >= 256:
        chunk = 256 if per % 256 == 0 else per
        return per, chunk, per // chunk, 1
    group = max(g for g in range(1, n_gene + 1) if n_gene % g == 0 and g * per <= 384 and (g * per) % LANES == 0)
    return per, per * group, 1, group


def kernel(
    n_gene,
    n_row,
    x_hbm,
    cell_hbm,
    index_hbm,
    scale_hbm,
    gene_hbm,
    first_hbm,
    second_hbm,
    rows_out,
    factor_out,
    first_out,
    second_out,
    cell_ref,
    index_ref,
    scale_ref,
    gene_ref,
    first_ref,
    second_ref,
    x_buf,
    fac,
    fac_t,
    gath,
    gath_t,
    cols,
    send_buf,
    recv_buf,
    own,
    col_send,
    col_recv,
    load_sem,
    x_sem,
    ag_send_sem,
    ag_recv_sem,
    send_sem,
    recv_sem,
    col_send_sem,
    col_recv_sem,
):
    rows, genes = x_buf.shape
    cells, rank = cell_ref.shape
    genes_own = gene_ref.shape[0]
    scale_k = 4.0 / math.sqrt(genes * n_gene)
    per, chunk, pieces, group = plan(rows, n_gene)
    n_chunk = rows // chunk
    own_chunks = pieces
    me_gene = lax.axis_index("gene")
    me_row = lax.axis_index("row")

    barrier = pltpu.get_barrier_semaphore()
    for step in range(1, n_row):
        pl.semaphore_signal(barrier, inc=1, device_id={"row": lax.rem(me_row + step, n_row)}, device_id_type=MESH)
    relay = n_gene == 4 and group == 1
    if relay:
        high, low = me_gene // 2, lax.rem(me_gene, 2)
        inner = high + low - 2 * high * low
        outer = 1 - inner

        def partner(mask):
            flipped_high = 1 - high if mask >= 2 else high
            flipped_low = 1 - low if mask % 2 == 1 else low
            return 2 * flipped_high + flipped_low

        for mask in (1, 2):
            pl.semaphore_signal(barrier, inc=1, device_id={"gene": partner(mask)}, device_id_type=MESH)

        @pl.when(inner == 1)
        def _():
            pl.semaphore_signal(barrier, inc=1, device_id={"gene": partner(3)}, device_id_type=MESH)

        arrivals = n_row - 1 + 2 + inner
    else:
        for step in range(1, n_gene):
            peer = lax.rem(me_gene + step, n_gene)
            pl.semaphore_signal(barrier, inc=1, device_id={"gene": peer}, device_id_type=MESH)
        arrivals = n_row - 1 + n_gene - 1

    if group == 1:
        first = me_gene * pieces + pieces
    else:
        first = me_gene // group + 1

    def chunk_at(i):
        if relay:
            return partner(3 - i // pieces) * pieces + i % pieces
        return lax.rem(first + i, n_chunk)

    def x_copy(i):
        window = pl.ds(pl.multiple_of(chunk_at(i) * chunk, chunk), chunk)
        return pltpu.make_async_copy(x_hbm.at[window], x_buf.at[pl.ds(i * chunk, chunk)], x_sem.at[i])

    loads = [
        pltpu.make_async_copy(src, dst, load_sem.at[k])
        for k, (src, dst) in enumerate(
            (
                (gene_hbm, gene_ref),
                (cell_hbm, cell_ref),
                (index_hbm, index_ref),
                (scale_hbm, scale_ref),
                (first_hbm, first_ref),
                (second_hbm, second_ref),
            )
        )
    ]
    for load in loads[:4]:
        load.start()
    for i in range(n_chunk):
        x_copy(i).start()
    for load in loads[4:]:
        load.start()

    loads[0].wait()
    own_genes = pl.ds(pl.multiple_of(me_row * genes_own, genes_own), genes_own)
    gath[own_genes] = gene_ref[...].astype(jnp.bfloat16)

    loads[1].wait()
    loads[2].wait()
    cell_t = cell_ref[...].astype(jnp.float32).T.astype(jnp.bfloat16)
    cell_id = lax.broadcasted_iota(jnp.int32, (cells, LANES), 0) + me_row * cells

    def gather_factors(c):
        parts = []
        for k in range(chunk // LANES):
            at = c * (chunk // LANES) + k
            hit = (cell_id == index_ref[pl.ds(at, 1), :]).astype(jnp.float32).astype(jnp.bfloat16)
            parts.append(jnp.dot(cell_t, hit, preferred_element_type=jnp.float32))
        both = jnp.concatenate(parts, axis=1)
        fac_t[c] = both.astype(jnp.bfloat16)
        fac[c] = both.T.astype(jnp.bfloat16)

    pl.semaphore_wait(barrier, arrivals)

    def ag_copy(step):
        peer = lax.rem(me_row + step, n_row)
        return pltpu.make_async_remote_copy(
            src_ref=gath.at[own_genes],
            dst_ref=gath.at[own_genes],
            send_sem=ag_send_sem.at[step - 1],
            recv_sem=ag_recv_sem.at[step - 1],
            device_id={"row": peer},
            device_id_type=MESH,
        )

    for step in range(1, n_row):
        ag_copy(step).start()
    for c in range(n_chunk):
        gather_factors(c)
    loads[3].wait()
    scale = jnp.concatenate([scale_ref[k : k + 1, :] for k in range(genes // LANES)], axis=1)
    inv = 1.0 / scale
    inv_tc = inv * (1.0 / tukey_c)
    inv_sq = inv * inv
    for step in range(1, n_row):
        ag_copy(step).wait()
    factor = gath[...]
    gath_t[...] = factor.astype(jnp.float32).T.astype(jnp.bfloat16)

    def block_copy(i, j):
        if relay:
            turn, piece = i // pieces, i % pieces
            target, slot = partner(3 - turn), turn
            if turn == 0:
                target, slot = outer * partner(1) + inner * target, 3 * outer
            return pltpu.make_async_remote_copy(
                src_ref=send_buf.at[i],
                dst_ref=recv_buf.at[slot, piece],
                send_sem=send_sem.at[i, 0],
                recv_sem=recv_sem.at[slot, piece],
                device_id={"gene": target},
                device_id_type=MESH,
            )
        c = chunk_at(i)
        owner = c // pieces if group == 1 else c * group + j
        piece = lax.rem(c, pieces) if group == 1 else 0
        size = chunk if group == 1 else per
        return pltpu.make_async_remote_copy(
            src_ref=send_buf.at[i, pl.ds(j * size, size)],
            dst_ref=recv_buf.at[me_gene, piece],
            send_sem=send_sem.at[i, j],
            recv_sem=recv_sem.at[me_gene, piece],
            device_id={"gene": owner},
            device_id_type=MESH,
        )

    def landed(slot, piece):
        pltpu.make_async_remote_copy(
            src_ref=recv_buf.at[slot, piece],
            dst_ref=recv_buf.at[slot, piece],
            send_sem=send_sem.at[0, 0],
            recv_sem=recv_sem.at[slot, piece],
            device_id={"gene": lax.rem(me_gene + 1, n_gene)},
            device_id_type=MESH,
        ).wait_recv()
        return recv_buf[slot, piece].astype(jnp.float32)

    for i in range(n_chunk):
        c = chunk_at(i)
        x_copy(i).wait()
        f = fac[c]
        pred = jnp.dot(f, gath_t[...], preferred_element_type=jnp.float32)
        resid = x_buf[i * chunk : (i + 1) * chunk].astype(jnp.float32) - pred
        ratio = resid * inv_tc
        inside = jnp.maximum(1.0 - ratio * ratio, 0.0)
        infl = (resid * inv_sq * (inside * inside)).astype(jnp.bfloat16)
        part = jnp.dot(infl, gath[...], preferred_element_type=jnp.float32)
        if group == 1 and i >= n_chunk - own_chunks:
            own[i - (n_chunk - own_chunks)] = part
        elif relay and i // pieces == 1:

            @pl.when(inner == 1)
            def _():
                send_buf[i] = (part + landed(3, i % pieces)).astype(jnp.bfloat16)

            @pl.when(inner == 0)
            def _():
                send_buf[i] = part.astype(jnp.bfloat16)

        else:
            send_buf[i] = part.astype(jnp.bfloat16)
            if group > 1:
                for j in range(group):

                    @pl.when(c * group + j == me_gene)
                    def _():
                        own[0] = part[j * per : (j + 1) * per]

        add = jnp.dot(fac_t[c], infl, preferred_element_type=jnp.float32)
        cols[...] = add if i == 0 else cols[...] + add
        if group == 1:
            if i < n_chunk - own_chunks:
                block_copy(i, 0).start()
        else:
            for j in range(group):

                @pl.when(c * group + j != me_gene)
                def _():
                    block_copy(i, j).start()

    total = cols[...].T
    col_send[...] = total.astype(jnp.bfloat16)
    cols_own = jnp.zeros((genes_own, rank), jnp.float32)

    def col_copy(step):
        peer = lax.rem(me_row + step, n_row)
        return pltpu.make_async_remote_copy(
            src_ref=col_send.at[pl.ds(pl.multiple_of(peer * genes_own, genes_own), genes_own)],
            dst_ref=col_recv.at[step - 1],
            send_sem=col_send_sem.at[step - 1],
            recv_sem=col_recv_sem.at[step - 1],
            device_id={"row": peer},
            device_id_type=MESH,
        )

    for step in range(1, n_row):
        col_copy(step).start()
    cols_own = col_send[own_genes].astype(jnp.float32)
    for step in range(1, n_row):
        col_copy(step).wait()
        cols_own = cols_own + col_recv[step - 1].astype(jnp.float32)
    loads[4].wait()
    loads[5].wait()
    grad_genes = -scale_k * cols_own
    new_first = beta_one * first_ref[...] + (1.0 - beta_one) * grad_genes
    new_second = beta_two * second_ref[...] + (1.0 - beta_two) * grad_genes * grad_genes
    first_hat = new_first / (1.0 - beta_one**10)
    second_hat = new_second / (1.0 - beta_two**10)
    first_out[...] = new_first
    second_out[...] = new_second
    factor_out[...] = gene_ref[...] - learn_rate * first_hat / (jnp.sqrt(second_hat) + adam_eps)

    size = chunk if group == 1 else per

    for piece in range(pieces):
        window = pl.ds(piece * size, size)
        acc = own[piece]
        if relay:
            acc = acc + landed(1, piece) + landed(2, piece)
            rows_out[window] = -scale_k * acc

            @pl.when(inner == 1)
            def _():
                rows_out[window] = -scale_k * (acc + landed(0, piece))
        else:
            for step in range(1, n_gene):
                acc = acc + landed(lax.rem(me_gene + n_gene - step, n_gene), piece)
            rows_out[window] = -scale_k * acc

    for i in range(n_chunk):
        if group == 1:
            if i < n_chunk - own_chunks:
                block_copy(i, 0).wait_send()
        else:
            for j in range(group):

                @pl.when(chunk_at(i) * group + j != me_gene)
                def _():
                    block_copy(i, j).wait_send()


def fused(n_gene, n_row, x_slab, cell_factor, index, scale, gene_factor, first, second):
    rows, genes = x_slab.shape
    cells, rank = cell_factor.shape
    genes_own = gene_factor.shape[0]
    per, chunk, pieces, group = plan(rows, n_gene)
    n_chunk = rows // chunk
    size = chunk if group == 1 else per
    vmem = pl.BlockSpec(memory_space=pltpu.VMEM)
    bf = jnp.bfloat16
    dma = pltpu.SemaphoreType.DMA
    return pl.pallas_call(
        functools.partial(kernel, n_gene, n_row),
        out_shape=(pltpu.VMEM((per, rank), jnp.float32),) + (pltpu.VMEM((genes_own, rank), jnp.float32),) * 3,
        in_specs=[pl.BlockSpec(memory_space=pl.ANY)] * 7,
        out_specs=(vmem,) * 4,
        scratch_shapes=[
            pltpu.VMEM(cell_factor.shape, bf),
            pltpu.VMEM(index.shape, jnp.int32),
            pltpu.VMEM(scale.shape, jnp.float32),
            pltpu.VMEM(gene_factor.shape, jnp.float32),
            pltpu.VMEM(gene_factor.shape, jnp.float32),
            pltpu.VMEM(gene_factor.shape, jnp.float32),
            pltpu.VMEM((rows, genes), bf),
            pltpu.VMEM((n_chunk, chunk, rank), bf),
            pltpu.VMEM((n_chunk, rank, chunk), bf),
            pltpu.VMEM((genes, rank), bf),
            pltpu.VMEM((rank, genes), bf),
            pltpu.VMEM((rank, genes), jnp.float32),
            pltpu.VMEM((n_chunk, chunk, rank), bf),
            pltpu.VMEM((n_gene, pieces, size, rank), bf),
            pltpu.VMEM((pieces, size, rank), jnp.float32),
            pltpu.VMEM((genes, rank), bf),
            pltpu.VMEM((n_row - 1, genes_own, rank), bf),
            dma((6,)),
            dma((n_chunk,)),
            dma((n_row - 1,)),
            dma((n_row - 1,)),
            dma((n_chunk, group)),
            dma((n_gene, pieces)),
            dma((n_row - 1,)),
            dma((n_row - 1,)),
        ],
        compiler_params=pltpu.CompilerParams(collective_id=0, has_side_effects=True),
    )(x_slab, cell_factor, index, scale, gene_factor, first, second)


def write_kernel(*refs):
    count = (len(refs) - 1) // 2
    sem = refs[-1]
    copies = [pltpu.make_async_copy(refs[k], refs[count + k], sem.at[k]) for k in range(count)]
    for copy in copies:
        copy.start()
    for copy in copies:
        copy.wait()


def write_out(held):
    return pl.pallas_call(
        write_kernel,
        out_shape=tuple(jax.ShapeDtypeStruct(h.shape, h.dtype) for h in held),
        in_specs=[pl.BlockSpec(memory_space=pltpu.VMEM)] * len(held),
        out_specs=(pl.BlockSpec(memory_space=pl.ANY),) * len(held),
        scratch_shapes=[pltpu.SemaphoreType.DMA((len(held),))],
    )(*[pltpu.with_memory_space_constraint(h, pltpu.VMEM) for h in held])


def local(x_slab, cell_factor, row_index, gene_scale, gene_factor, first_moment, second_moment):
    rows_dev, genes_dev = x_slab.shape
    n_gene = lax.axis_size("gene")
    n_row = lax.axis_size("row")
    held = fused(
        n_gene,
        n_row,
        x_slab,
        cell_factor,
        row_index.reshape(rows_dev // LANES, LANES),
        gene_scale.reshape(genes_dev // LANES, LANES),
        gene_factor,
        first_moment,
        second_moment,
    )
    return write_out(held)


def solution(mesh):
    in_specs = (
        P(("grp", "row"), "gene"),
        P(("grp", "row"), None),
        P(("grp", "row")),
        P(("grp", "gene")),
        P(("grp", "gene", "row"), None),
        P(("grp", "gene", "row"), None),
        P(("grp", "gene", "row"), None),
    )
    out_specs = (
        P(("grp", "row", "gene"), None),
        P(("grp", "gene", "row"), None),
        P(("grp", "gene", "row"), None),
        P(("grp", "gene", "row"), None),
    )
    return jax.shard_map(local, mesh=mesh, in_specs=in_specs, out_specs=out_specs, check_vma=False)
```
